512 devices in a mesh: seq: 16 (over z_lo, core), tp: 8 (over z_hi, y), rep: 4 (over x).
Axes of the slice: x: 4, y: 4, z: 16 (z_hi: 2, z_lo: 8; z = z_hi * 8 + z_lo), core: 2. Of those that a mesh axis runs over, the one named last changes fastest.
Arguments:
- counts: int32 [4, 16], P('rep'), may hold values from 1 to 40, 256 in all within a row
- prompt_of: int32 [4, 256], P('rep'), may hold values from 0 to 7, as said below
- queries: bfloat16 [4, 640, 8192], P('rep', 'seq', 'tp'), may hold values from -10 to 10
- new_kv: bfloat16 [4, 640, 2, 1024], P('rep', 'seq', None, 'tp'), may hold values from -10 to 10
- prompt_keys: bfloat16 [4, 8, 16384, 1024], P('rep', None, 'seq', 'tp'), may hold values from -6 to 6
- prompt_values: bfloat16 [4, 8, 16384, 1024], P('rep', None, 'seq', 'tp'), may hold values from -6 to 6
- suffix_keys: bfloat16 [4, 256, 64, 1024], P('rep', 'seq', None, 'tp'), may hold values from -9 to 9
- suffix_values: bfloat16 [4, 256, 64, 1024], P('rep', 'seq', None, 'tp'), may hold values from -6 to 6
- gen_len: int32 [4, 256], P('rep', 'seq'), may hold values from 1 to 64, 8192 in all within a row
- out_weight: bfloat16 [8192, 8192], P('tp', ('seq', 'rep')), may hold values from -0.0625 to 0.0625
Outputs:
- projected: bfloat16 [1024, 8192], P('tp', ('seq', 'rep'))
The draws below stay inside these ranges and needn't reach their ends.
Inputs may be any that keep to these rules, and one draw needn't show every extreme that they name: In each group the live slots of seq index s are its first counts[s] slots; together they hold the group's rows in order. `prompt_of`: in each group every prompt is named by exactly 32 rows.
All inputs are finite; a program needn't handle non-finite values. No bound on the sum of `gen_len` on one device may be relied on, other than what follows from the above.
Results may differ from the reference program's by a relative error of at most 0.014.
Values may be sent and summed in bfloat16 or wider, within the bound.
No kernel may reach another device: no remote copies, remote signals or barrier semaphores. Data moves between devices by JAX's collectives and lax.ppermute only.
A program may use at most 128 MiB of HBM per device.

```python
import math
import jax
import jax.numpy as jnp
import numpy as np
from jax import lax

D = 8192
HEADS = 64
KV_HEADS = 8
HD = 128
ANSWERS = 32
P_GRP = 8
PROMPT_DEV = 1024
SUF_MAX = 64
ROWS_GRP = 256
CAP = 40
PROMPT_LEN = 16384
N_SEQ = 16
N_REP = 4


def draw_prompt_of(key, part):
    rows = P_GRP * ANSWERS
    keys = jax.random.split(jax.random.fold_in(key, 77), N_REP)
    orders = jax.vmap(lambda one: jax.random.permutation(one, rows))(keys)
    return (orders // ANSWERS).astype(jnp.int32)


def draw_queries(key, part):
    slots = N_SEQ * CAP
    shape = (N_REP, slots, HEADS * HD)
    return jnp.clip(2.5 * jax.random.normal(jax.random.fold_in(key, 1), shape, jnp.float32), -10.0, 10.0).astype(jnp.bfloat16)


def draw_prompt_keys(key, part):
    length = PROMPT_DEV * N_SEQ
    shape = (N_REP, P_GRP, length, KV_HEADS * HD)
    return jnp.clip(jax.random.normal(jax.random.fold_in(key, 5), shape, jnp.float32), -6.0, 6.0).astype(jnp.bfloat16)


def shard_levels(rng, extent, shards, low, high):
    def one(dim, shards_of):
        heights = jax.random.uniform(jax.random.fold_in(jax.random.fold_in(rng, 6), dim), (shards_of,), jnp.float32, low / len(shards), high / len(shards))
        return jnp.repeat(jnp.exp(heights), extent[dim] // shards_of).reshape((-1,) + (1,) * (len(extent) - dim - 1))

    gain = one(*shards[0])
    for cut in shards[1:]:
        gain = gain * one(*cut)
    return gain


def split_up(amount, total, bound, lean):
    weights = [(1 << 20) // math.isqrt(standing ** lean) + 1 for standing in range(2, amount + 1)]
    rest, given = total - bound - (amount - 1), [1] * (amount - 1)
    while rest > 0:
        free = [i for i in range(amount - 1) if given[i] < bound]
        mass, left = sum([weights[i] for i in free]), rest
        for i in free:
            addition = min(bound - given[i], max(1, left * weights[i] // mass), rest)
            given[i] = given[i] + addition
            rest = rest - addition
    return np.array([bound] + given)


def uneven_parts(own_key, number_of, total, reach, lean):
    if number_of == 2:
        one = jax.random.randint(own_key, (), max(1, total - reach), min(reach, total - 1) + 1)
        return jnp.stack([one, total - one])
    tallies = jnp.asarray(split_up(number_of, total, reach, lean), jnp.int32)
    pairs = (number_of - 1) // 2
    donor, taker = tallies[1:1 + 2 * pairs:2], tallies[2:2 + 2 * pairs:2]
    room = jnp.minimum(donor - 1, reach - taker)
    moved = jax.random.randint(jax.random.fold_in(own_key, 1), (pairs,), 0, 1 << 20) % (room + 1)
    tallies = tallies.at[1:1 + 2 * pairs:2].set(donor - moved).at[2:2 + 2 * pairs:2].set(taker + moved)
    return tallies[jax.random.permutation(jax.random.fold_in(own_key, 2), number_of)]


def normal_values(own_key, shape, spread, bound, cuts=(), kind=jnp.bfloat16):
    result = jax.random.normal(own_key, shape, jnp.float32) * spread
    if len(cuts) > 0:
        result = shard_levels(own_key, shape, cuts, -0.22, 0.18) * result
    return jnp.clip(result, min=-bound, max=bound).astype(kind)


def setup_inputs(seed: int = 0) -> dict:
    splits = jax.random.split(jax.random.key(seed), 11)
    counts = jax.vmap(lambda own: uneven_parts(own, N_SEQ, ROWS_GRP, CAP, 2))(jax.random.split(splits[0], N_REP)).reshape((N_REP, N_SEQ)).astype(jnp.int32)
    prompt_of = draw_prompt_of(jax.random.fold_in(splits[10], 71), 0)
    queries = draw_queries(jax.random.fold_in(splits[10], 71), 0)
    new_kv = normal_values(splits[3], (N_REP, N_SEQ * CAP, 2, KV_HEADS * HD), 2.0, 10.0, ((0, 4), (1, 16), (3, 8)))
    prompt_keys = draw_prompt_keys(jax.random.fold_in(splits[10], 71), 0)
    prompt_values = normal_values(splits[5], (N_REP, P_GRP, PROMPT_LEN, KV_HEADS * HD), 1.0, 6.0, ((0, 4), (2, 16), (3, 8)))
    suffix_keys = normal_values(splits[6], (N_REP, ROWS_GRP, SUF_MAX, KV_HEADS * HD), 1.5, 9.0, ((0, 4), (1, 16), (3, 8)))
    suffix_values = normal_values(splits[7], (N_REP, ROWS_GRP, SUF_MAX, KV_HEADS * HD), 1.0, 6.0, ((0, 4), (1, 16), (3, 8)))
    gen_len = jax.vmap(lambda own: uneven_parts(own, ROWS_GRP, ROWS_GRP * SUF_MAX // 2, SUF_MAX, 1))(jax.random.split(splits[8], N_REP)).reshape((N_REP, ROWS_GRP)).astype(jnp.int32)
    out_weight = normal_values(splits[9], (HEADS * HD, D), (HEADS * HD) ** -0.5, 0.0625, ((0, 8), (1, 64)))
    return dict(counts=counts, prompt_of=prompt_of, queries=queries, new_kv=new_kv, prompt_keys=prompt_keys, prompt_values=prompt_values, suffix_keys=suffix_keys, suffix_values=suffix_values, gen_len=gen_len, out_weight=out_weight)


def reference(counts, prompt_of, queries, new_kv, prompt_keys, prompt_values, suffix_keys, suffix_values, gen_len, out_weight):
    scale = HD ** -0.5
    share = HEADS // KV_HEADS
    pieces = []
    for group in range(N_REP):
        tally = counts[group].astype(jnp.int32)
        ends = jnp.cumsum(tally).astype(jnp.int32)
        starts = (ends - tally).astype(jnp.int32)
        row_ids = jnp.arange(ROWS_GRP, dtype=jnp.int32)
        holder = jnp.sum((ends[None, :] <= row_ids[:, None]).astype(jnp.int32), axis=1).astype(jnp.int32)
        slot_ids = (holder * CAP + row_ids - starts[holder]).astype(jnp.int32)
        row_queries = queries[group][slot_ids]
        row_kv = new_kv[group][slot_ids]
        group_keys = prompt_keys[group]
        group_values = prompt_values[group]

        def one_row(items):
            query, fresh, prompt, cache_k, cache_v, length = items
            keys = jnp.concatenate([lax.dynamic_index_in_dim(group_keys, prompt, 0, keepdims=False), cache_k, fresh[0][None, :]], axis=0)
            values = jnp.concatenate([lax.dynamic_index_in_dim(group_values, prompt, 0, keepdims=False), cache_v, fresh[1][None, :]], axis=0)
            query_f = query.astype(jnp.float32).reshape(KV_HEADS, share, HD)
            keys_f = keys.astype(jnp.float32).reshape(-1, KV_HEADS, HD)
            values_f = values.astype(jnp.float32).reshape(-1, KV_HEADS, HD)
            scores = jnp.einsum("kgd,lkd->kgl", query_f, keys_f) * scale
            valid = jnp.concatenate([jnp.ones((PROMPT_LEN,), bool), jnp.arange(SUF_MAX, dtype=jnp.int32) < length, jnp.ones((1,), bool)])
            scores = jnp.where(valid[None, None, :], scores, -jnp.inf)
            peak = jnp.max(scores, axis=-1, keepdims=True)
            weights = jnp.exp(scores - peak)
            total = jnp.sum(weights, axis=-1)
            rounded = lax.optimization_barrier(weights.astype(jnp.bfloat16)).astype(jnp.float32)
            mixed = jnp.einsum("kgl,lkd->kgd", rounded, values_f)
            return (mixed / total[..., None]).reshape(HEADS * HD).astype(jnp.bfloat16)

        attended = lax.map(one_row, (row_queries, row_kv, prompt_of[group].astype(jnp.int32), suffix_keys[group], suffix_values[group], gen_len[group].astype(jnp.int32)))
        pieces.append(attended)
    every_row = jnp.concatenate(pieces, axis=0)
    return jnp.dot(every_row, out_weight, preferred_element_type=jnp.float32).astype(jnp.bfloat16)
```

```python
import functools
import math

import jax
import jax.numpy as jnp
from jax import lax
from jax.experimental import pallas as pl
from jax.experimental.pallas import tpu as pltpu
from jax.sharding import PartitionSpec as P

HD = 128
LANES = 128
NEG = -1e30
BF = jnp.bfloat16
F32 = jnp.float32


def swap(x, axis, bit):
    size = lax.axis_size(axis)
    return lax.ppermute(x, axis, [(i, i ^ bit) for i in range(size)])


def dot(a, b):
    return lax.dot_general(a, b, (((1,), (0,)), ((), ())), preferred_element_type=F32)


def dot_t(a, b):
    return lax.dot_general(a, b, (((1,), (1,)), ((), ())), preferred_element_type=F32)


def split_stats(stat):
    hi = stat.astype(BF).astype(F32)
    rest = stat - hi
    mid = rest.astype(BF).astype(F32)
    low = rest - mid
    lane = lax.broadcasted_iota(jnp.int32, stat.shape, 1)
    out = jnp.where(lane < 8, hi, jnp.where(lane < 16, pltpu.roll(mid, 8, 1), pltpu.roll(low, 16, 1)))
    return jnp.where(lane < 24, out, 0.0).astype(BF)


def join_stats(packed):
    x = packed.astype(F32)
    return x + pltpu.roll(x, LANES - 8, 1) + pltpu.roll(x, LANES - 16, 1)


def heads_down(x, heads):
    return jnp.concatenate([x[:, h * HD : (h + 1) * HD] for h in range(heads)], axis=0)


def lanes_of(column, heads, rows):
    lane = lax.broadcasted_iota(jnp.int32, (rows, LANES), 1)
    out = jnp.zeros((rows, LANES), F32)
    for h in range(heads):
        out = jnp.where(lane == h, column[h * rows : (h + 1) * rows], out)
    return out


def one_hot(ids, width, offset=0):
    lane = lax.broadcasted_iota(jnp.int32, (ids.shape[0], width), 1)
    return jnp.where(ids - offset == lane, 1.0, 0.0).astype(BF)


def attend_kernel(heads, scalars, spos, dest, own_pos, gens, near, far, new_k, new_v, keys, values, suf_k, suf_v, keep, send, sorted_rows):
    step = pl.program_id(0)
    width = heads * HD
    half = near.shape[0]
    factor = HD**-0.5 * math.log2(math.e)

    def pick(ids):
        q = dot(one_hot(ids, half), near[...]) + dot(one_hot(ids, half, half), far[...])
        return heads_down(q.astype(BF), heads)

    ids = spos[...]
    rows = ids.shape[0]
    q = pick(ids)
    fresh = one_hot(ids, new_k.shape[0])
    fresh_k = jnp.concatenate([dot(fresh, new_k[...])] * heads, axis=0)
    fresh_v = jnp.concatenate([dot(fresh, new_v[...])] * heads, axis=0)
    mine = jnp.concatenate([ids] * heads, axis=0) < new_k.shape[0]
    self_score = jnp.sum(q.astype(F32) * fresh_k, axis=1, keepdims=True)
    self_score = jnp.where(mine, self_score, NEG)
    scores = dot_t(q, keys[0])
    peak = jnp.maximum(jnp.max(scores, axis=1, keepdims=True), self_score)
    weights = jnp.exp2((scores - peak) * factor)
    self_weight = jnp.exp2((self_score - peak) * factor)
    mass = jnp.sum(weights, axis=1, keepdims=True) + self_weight
    mixed = dot(weights.astype(BF), values[0]) + self_weight.astype(BF).astype(F32) * fresh_v
    mixed = (mixed / mass).astype(BF)
    at = pl.ds(pl.multiple_of(step * rows, rows), rows)
    for h in range(heads):
        sorted_rows[at, h * HD : (h + 1) * HD] = mixed[h * rows : (h + 1) * rows]
    stat = lanes_of(peak * factor + jnp.log2(mass), heads, rows)
    sorted_rows[at, width : width + LANES] = split_stats(stat)

    @pl.when(step == pl.num_programs(0) - 1)
    def _():
        total = sorted_rows.shape[0]
        place = lax.broadcasted_iota(jnp.int32, (total, total), 0)
        to_dest = jnp.where(place == dest[...], 1.0, 0.0).astype(BF)
        placed = dot(to_dest, sorted_rows[...]).astype(BF)
        keep[...] = placed[: total // 2]
        send[...] = placed[total // 2 :]
        own = own_pos.shape[0]
        qs = pick(own_pos[...])
        suffix = dot_t(qs, suf_k[...])
        depth = suf_k.shape[0] // own
        row = lax.broadcasted_iota(jnp.int32, suffix.shape, 0) % own
        col = lax.broadcasted_iota(jnp.int32, suffix.shape, 1)
        length = jnp.concatenate([gens[...]] * heads, axis=0)
        live = (col // depth == row) & (col % depth < length)
        suffix = jnp.where(live, suffix, NEG)
        top = jnp.max(suffix, axis=1, keepdims=True)
        w = jnp.where(live, jnp.exp2((suffix - top) * factor), 0.0)
        m = jnp.sum(w, axis=1, keepdims=True)
        o = dot(w.astype(BF), suf_v[...]) / m
        stat_s = lanes_of(top * factor + jnp.log2(m), heads, own)
        here = pl.ds(pl.multiple_of(scalars[0], own), own)
        old = keep[here, :]
        stat_p = join_stats(old[:, width : width + LANES])
        both = jnp.maximum(stat_p, stat_s)
        e_p, e_s = jnp.exp2(stat_p - both), jnp.exp2(stat_s - both)
        t = e_p + e_s
        f_p, f_s = e_p / t, e_s / t
        for h in range(heads):
            cut = slice(h * HD, (h + 1) * HD)
            keep[here, cut] = (
                old[:, cut].astype(F32) * f_p[:, h : h + 1] + o[h * own : (h + 1) * own] * f_s[:, h : h + 1]
            ).astype(BF)
        keep[here, width : width + LANES] = split_stats(both + jnp.log2(t))


def join_kernel(heads, parts, last, *refs):
    a, b = refs[:2]
    outs = refs[2:]
    width = heads * HD
    sa = join_stats(a[:, width : width + LANES])
    sb = join_stats(b[:, width : width + LANES])
    both = jnp.maximum(sa, sb)
    ea, eb = jnp.exp2(sa - both), jnp.exp2(sb - both)
    t = ea + eb
    fa, fb = ea / t, eb / t
    n = a.shape[0] // parts
    for h in range(heads):
        cut = slice(h * HD, (h + 1) * HD)
        o = (a[:, cut].astype(F32) * fa[:, h : h + 1] + b[:, cut].astype(F32) * fb[:, h : h + 1]).astype(BF)
        for i in range(parts):
            outs[i][:, cut] = o[i * n : (i + 1) * n]
    if not last:
        packed = split_stats(both + jnp.log2(t))
        for i in range(parts):
            outs[i][:, width : width + LANES] = packed[i * n : (i + 1) * n]


def join(a, b, heads, parts=1, last=False):
    n = a.shape[0] // parts
    cols = heads * HD if last else a.shape[1]
    return pl.pallas_call(
        functools.partial(join_kernel, heads, parts, last),
        out_shape=[jax.ShapeDtypeStruct((n, cols), BF)] * parts,
        in_specs=[pl.BlockSpec(memory_space=pltpu.VMEM)] * 2,
        out_specs=[pl.BlockSpec(memory_space=pltpu.VMEM)] * parts,
        name="join",
    )(a, b)


def project_kernel(groups, own, scalars, mine, other, weight, out):
    z_bit, core = scalars[1], scalars[2]
    for rel, ref in ((0, mine), (1, other)):
        y = dot(ref[...], weight[...]).astype(BF)
        at = 0
        for g in range(groups):
            for z_rel in range(2):
                for high in range(2):
                    for mid in range(2):
                        block = mid * 4 + (z_bit ^ z_rel) * 2 + (core ^ rel)
                        out[2 * g + high, block] = y[at : at + own]
                        at += own


def body(counts, prompt_of, queries, new_kv, prompt_keys, prompt_values, suffix_keys, suffix_values, gen_len, out_weight):
    me = lax.axis_index("seq")
    capacity, width = queries.shape[1:]
    heads = width // HD
    per_device = gen_len.shape[1]
    seq_count = lax.axis_size("seq")
    total = per_device * seq_count
    prompts, depth = prompt_keys.shape[1:3]
    block = total // prompts
    groups = lax.axis_size("rep")

    slots = queries[0]
    for bit in (8, 4, 2):
        slots = jnp.concatenate([slots, swap(slots, "seq", bit)], axis=0)
    others = swap(slots, "seq", 1)

    tally = counts[0]
    ends = jnp.cumsum(tally)
    row = jnp.arange(total, dtype=jnp.int32)
    past = ends[None, :] <= row[:, None]
    holder = jnp.sum(past.astype(jnp.int32), axis=1)
    offset = row - jnp.sum(jnp.where(past, tally[None, :], 0), axis=1)
    far = holder ^ me
    slot = (((far >> 3) & 1) + ((far >> 2) & 1) * 2 + ((far >> 1) & 1) * 4 + (far & 1) * 8) * capacity + offset
    device = row // per_device
    away = device ^ me
    dest = (
        (away & 1) * (total // 2)
        + ((away >> 1) & 1) * (total // 4)
        + (((device >> 2) & 1) + ((device >> 3) & 1) * 2) * per_device
        + row % per_device
    )
    prompt = prompt_of[0]
    before = (prompt[None, :] == prompt[:, None]) & (row[None, :] < row[:, None])
    rank = prompt * block + jnp.sum(before.astype(jnp.int32), axis=1)
    at_rank = rank[None, :] == row[:, None]
    slot_sorted = jnp.sum(jnp.where(at_rank, slot[None, :], 0), axis=1)
    dest_sorted = jnp.sum(jnp.where(at_rank, dest[None, :], 0), axis=1)
    own_slot = lax.dynamic_slice_in_dim(slot, me * per_device, per_device, 0)
    own_place = (((me >> 2) & 1) + ((me >> 3) & 1) * 2) * per_device
    scalars = jnp.stack([own_place, (me >> 1) & 1, me & 1, me]).astype(jnp.int32)

    packed = width + LANES
    half = slots.shape[0]
    whole = lambda *shape: pl.BlockSpec(shape, lambda i, s: (0,) * len(shape))
    keep, send = pl.pallas_call(
        functools.partial(attend_kernel, heads),
        out_shape=[jax.ShapeDtypeStruct((total // 2, packed), BF)] * 2,
        grid_spec=pltpu.PrefetchScalarGridSpec(
            num_scalar_prefetch=1,
            grid=(prompts,),
            in_specs=[
                pl.BlockSpec((block, 1), lambda i, s: (i, 0)),
                whole(1, total),
                whole(per_device, 1),
                whole(per_device, 1),
                whole(half, width),
                whole(half, width),
                whole(capacity, HD),
                whole(capacity, HD),
                pl.BlockSpec((1, depth, HD), lambda i, s: (i, 0, 0)),
                pl.BlockSpec((1, depth, HD), lambda i, s: (i, 0, 0)),
                whole(per_device * suffix_keys.shape[2], HD),
                whole(per_device * suffix_keys.shape[2], HD),
            ],
            out_specs=[whole(total // 2, packed)] * 2,
            scratch_shapes=[pltpu.VMEM((total, packed), BF)],
        ),
        name="attend",
    )(
        scalars,
        slot_sorted[:, None],
        dest_sorted[None, :],
        own_slot[:, None],
        gen_len[0][:, None],
        slots,
        others,
        new_kv[0, :, 0],
        new_kv[0, :, 1],
        prompt_keys[0],
        prompt_values[0],
        suffix_keys[0].reshape(-1, HD),
        suffix_values[0].reshape(-1, HD),
    )
    keep, send = join(keep, swap(send, "seq", 1), heads, parts=2)
    (part,) = join(keep, swap(send, "seq", 2), heads)
    (part,) = join(part, swap(part, "seq", 4), heads)
    (attended,) = join(part, swap(part, "seq", 8), heads, last=True)
    attended = jnp.concatenate([attended, swap(attended, "seq", 2)], axis=0)
    spread = jnp.broadcast_to(attended[None], (groups,) + attended.shape)
    every = lax.all_to_all(spread, "rep", 0, 0, tiled=True).reshape(-1, width)
    partner = swap(every, "seq", 1)
    tp = lax.axis_size("tp")
    partial_sums = pl.pallas_call(
        functools.partial(project_kernel, groups, per_device),
        out_shape=jax.ShapeDtypeStruct((tp, total // 2 // per_device, per_device, out_weight.shape[1]), BF),
        in_specs=[pl.BlockSpec(memory_space=pltpu.SMEM)] + [pl.BlockSpec(memory_space=pltpu.VMEM)] * 3,
        out_specs=pl.BlockSpec(memory_space=pltpu.VMEM),
        name="project",
    )(scalars, every, partner, out_weight)
    gathered = lax.all_to_all(partial_sums, "tp", 0, 0, tiled=True)
    summed = jnp.sum(gathered.astype(F32), axis=0).astype(BF)
    return summed.reshape(-1, out_weight.shape[1])


def solution(mesh):
    in_specs = (
        P("rep", None),
        P("rep", None),
        P("rep", "seq", "tp"),
        P("rep", "seq", None, "tp"),
        P("rep", None, "seq", "tp"),
        P("rep", None, "seq", "tp"),
        P("rep", "seq", None, "tp"),
        P("rep", "seq", None, "tp"),
        P("rep", "seq"),
        P("tp", ("seq", "rep")),
    )
    out_specs = P("tp", ("seq", "rep"))
    return jax.shard_map(body, mesh=mesh, in_specs=in_specs, out_specs=out_specs, check_vma=False)
```

```python
import functools
import math

import jax
import jax.numpy as jnp
from jax import lax
from jax.experimental import pallas as pl
from jax.experimental.pallas import tpu as pltpu
from jax.sharding import PartitionSpec as P


HD = 128
LANES = 128
NEG = -1e30
BF = jnp.bfloat16
F32 = jnp.float32


def swap(x, axis, bit):
    size = lax.axis_size(axis)
    return lax.ppermute(x, axis, [(i, i ^ bit) for i in range(size)])


def dot(a, b):
    return lax.dot_general(a, b, (((1,), (0,)), ((), ())), preferred_element_type=F32)


def dot_t(a, b):
    return lax.dot_general(a, b, (((1,), (1,)), ((), ())), preferred_element_type=F32)


def split_stats(stat):
    hi = stat.astype(BF).astype(F32)
    rest = stat - hi
    mid = rest.astype(BF).astype(F32)
    low = rest - mid
    lane = lax.broadcasted_iota(jnp.int32, stat.shape, 1)
    out = jnp.where(lane < 8, hi, jnp.where(lane < 16, pltpu.roll(mid, 8, 1), pltpu.roll(low, 16, 1)))
    return jnp.where(lane < 24, out, 0.0).astype(BF)


def join_stats(packed):
    x = packed.astype(F32)
    return x + pltpu.roll(x, LANES - 8, 1) + pltpu.roll(x, LANES - 16, 1)


def heads_down(x, heads):
    return jnp.concatenate([x[:, h * HD : (h + 1) * HD] for h in range(heads)], axis=0)


def lanes_of(column, heads, rows):
    lane = lax.broadcasted_iota(jnp.int32, (rows, LANES), 1)
    out = jnp.zeros((rows, LANES), F32)
    for h in range(heads):
        out = jnp.where(lane == h, column[h * rows : (h + 1) * rows], out)
    return out


def one_hot(ids, width, offset=0):
    lane = lax.broadcasted_iota(jnp.int32, (ids.shape[0], width), 1)
    return jnp.where(ids - offset == lane, 1.0, 0.0).astype(BF)


def log_stats(top, mass, factor, heads, rows):
    return split_stats(lanes_of(top * factor + jnp.log2(mass), heads, rows))


def attend_kernel(heads, pairs, core, spos, dest, own_pos, gens, slots, new_kv, keys, other_keys, values, other_values, suf, out, suffix_out, sorted_rows):
    step = pl.program_id(0)
    width = heads * HD
    factor = HD**-0.5 * math.log2(math.e)

    def pick(ids):
        q = dot(one_hot(ids, slots.shape[0]), slots[...])
        return heads_down(q.astype(BF), heads)

    rows = spos.shape[0] // pairs
    for pair in range(pairs):
        ids = spos[pair * rows : (pair + 1) * rows]
        q = pick(ids)
        fresh = dot(one_hot(ids, new_kv.shape[0]), new_kv[...])
        fresh_k = jnp.concatenate([fresh[:, :HD]] * heads, axis=0)
        fresh_v = jnp.concatenate([fresh[:, HD:]] * heads, axis=0)
        mine = jnp.concatenate([ids] * heads, axis=0) < new_kv.shape[0]
        self_score = jnp.sum(q.astype(F32) * fresh_k, axis=1, keepdims=True)
        self_score = jnp.where(mine, self_score, NEG)
        near = dot_t(q, keys[pair])
        far = dot_t(q, other_keys[pair])
        peak = jnp.maximum(jnp.max(near, axis=1, keepdims=True), jnp.max(far, axis=1, keepdims=True))
        peak = jnp.maximum(peak, self_score)
        near = jnp.exp2((near - peak) * factor)
        far = jnp.exp2((far - peak) * factor)
        self_weight = jnp.exp2((self_score - peak) * factor)
        mass = jnp.sum(near, axis=1, keepdims=True) + jnp.sum(far, axis=1, keepdims=True) + self_weight
        mixed = dot(near.astype(BF), values[pair]) + dot(far.astype(BF), other_values[pair])
        mixed = mixed + self_weight.astype(BF).astype(F32) * fresh_v
        mixed = (mixed / mass).astype(BF)
        at = pl.ds(pl.multiple_of((step * pairs + pair) * rows, rows), rows)
        for h in range(heads):
            sorted_rows[at, h * HD : (h + 1) * HD] = mixed[h * rows : (h + 1) * rows]
        sorted_rows[at, width : width + LANES] = log_stats(peak, mass, factor, heads, rows)

    @pl.when(step == 0)
    def _():
        own = own_pos.shape[0] // 2
        tall = suf.shape[0] // 4
        for rel in range(2):
            qs = pick(own_pos[rel * own : (rel + 1) * own])
            base = rel * 2 * tall
            score = dot_t(qs, suf[base : base + tall])
            depth = tall // own
            row = lax.broadcasted_iota(jnp.int32, score.shape, 0) % own
            col = lax.broadcasted_iota(jnp.int32, score.shape, 1)
            length = jnp.concatenate([gens[rel * own : (rel + 1) * own]] * heads, axis=0)
            live = (col // depth == row) & (col % depth < length)
            score = jnp.where(live, score, NEG)
            top = jnp.max(score, axis=1, keepdims=True)
            w = jnp.where(live, jnp.exp2((score - top) * factor), 0.0)
            m = jnp.sum(w, axis=1, keepdims=True)
            o = (dot(w.astype(BF), suf[base + tall : base + 2 * tall]) / m).astype(BF)
            at = pl.ds(pl.multiple_of((core[0] ^ rel) * own, own), own)
            for h in range(heads):
                suffix_out[at, h * HD : (h + 1) * HD] = o[h * own : (h + 1) * own]
            suffix_out[at, width : width + LANES] = log_stats(top, m, factor, heads, own)

    @pl.when(step == pl.num_programs(0) - 1)
    def _():
        total = sorted_rows.shape[0]
        place = lax.broadcasted_iota(jnp.int32, (total, total), 0)
        to_dest = jnp.where(place == dest[...], 1.0, 0.0).astype(BF)
        placed = dot(to_dest, sorted_rows[...]).astype(BF)
        n = out.shape[1]
        for i in range(out.shape[0]):
            out[i] = placed[i * n : (i + 1) * n]


def join_kernel(heads, parts, suffix, out):
    width = heads * HD
    count = parts.shape[0]
    stats = [join_stats(parts[i, :, width : width + LANES]) for i in range(count)]
    stats.append(join_stats(suffix[:, width : width + LANES]))
    top = functools.reduce(jnp.maximum, stats)
    grown = [jnp.exp2(s - top) for s in stats]
    total = functools.reduce(jnp.add, grown)
    share = [e / total for e in grown]
    for h in range(heads):
        cut = slice(h * HD, (h + 1) * HD)
        o = suffix[:, cut].astype(F32) * share[count][:, h : h + 1]
        for i in range(count):
            o = o + parts[i, :, cut].astype(F32) * share[i][:, h : h + 1]
        o = o.astype(BF)
        for i in range(out.shape[0]):
            out[i, :, cut] = o


def project_kernel(spot, mine, partner, w0, w1, w2, w3, out):
    core, group = spot[0], spot[1]
    out[...] = jnp.zeros_like(out)
    depth = mine.shape[1]
    near = pl.ds(pl.multiple_of(core * depth, depth), depth)
    far = pl.ds(pl.multiple_of((1 - core) * depth, depth), depth)
    n = out.shape[1]
    for rel, w in enumerate((w0, w1, w2, w3)):
        y = (dot(mine[...], w[near, :]) + dot(partner[...], w[far, :])).astype(BF)
        for high in range(2):
            out[((group % 2) * 2 + high) * 4 + (group ^ rel)] = y[high * n : (high + 1) * n]


def plane_kernel(spot, parts, keep, send):
    sums = []
    for top in range(2):
        terms = [parts[y * 4 + top * 2 + g].astype(F32) for y in range(4) for g in range(2)]
        sums.append(functools.reduce(jnp.add, terms))
    upper = spot[2] == 1
    keep[...] = jnp.where(upper, sums[1], sums[0])
    send[...] = jnp.where(upper, sums[0], sums[1]).astype(BF)


VMEM = pl.BlockSpec(memory_space=pltpu.VMEM)
SMEM = pl.BlockSpec(memory_space=pltpu.SMEM)


def body(counts, prompt_of, queries, new_kv, prompt_keys, prompt_values, suffix_keys, suffix_values, gen_len, out_weight):
    me = lax.axis_index("seq")
    core, chip = me & 1, me >> 1
    group = lax.axis_index("rep")
    upper = lax.axis_index("tp") >> 2
    capacity, width = queries.shape[1:]
    heads = width // HD // 2
    half = heads * HD
    per_device = gen_len.shape[1]
    seq_count = lax.axis_size("seq")
    chips = seq_count // 2
    total = per_device * seq_count
    prompts, depth = prompt_keys.shape[1:3]
    block = total // prompts
    line = [[2 * i + c for i in range(chips)] for c in range(2)]

    halves = queries[0][:, :half], queries[0][:, half:]
    low = core == 0
    mine = jnp.where(low, halves[0], halves[1])
    theirs = jnp.where(low, halves[1], halves[0])
    slots = jnp.concatenate([mine, swap(theirs, "seq", 1)], axis=0)

    small = jnp.concatenate(
        [
            new_kv[0].reshape(capacity, 2 * HD),
            jnp.broadcast_to(gen_len[0].astype(BF)[:, None], (per_device, 2 * HD)),
        ],
        axis=0,
    )
    suffix = jnp.concatenate([suffix_keys[0].reshape(-1, HD), suffix_values[0].reshape(-1, HD)], axis=0)
    slots, small, suffix, keys, values, weight = lax.optimization_barrier(
        (slots, small, suffix, prompt_keys[0], prompt_values[0], out_weight)
    )
    for bit in (8, 4, 2):
        slots = jnp.concatenate([slots, swap(slots, "seq", bit)], axis=0)
    other_small = swap(small, "seq", 1)
    other_suffix = swap(suffix, "seq", 1)
    other_keys = swap(keys, "seq", 1)
    other_values = swap(values, "seq", 1)
    weights = [weight] + [swap(weight, "rep", bit) for bit in (1, 2, 3)]

    new_pairs = jnp.concatenate([small[:capacity], other_small[:capacity]], axis=0)
    gens = jnp.concatenate([small[capacity:, :1], other_small[capacity:, :1]], axis=0).astype(jnp.int32)
    suffixes = jnp.concatenate([suffix, other_suffix], axis=0)

    tally = counts[0]
    ends = jnp.cumsum(tally)
    row = jnp.arange(total, dtype=jnp.int32)
    past = ends[None, :] <= row[:, None]
    holder = jnp.sum(past.astype(jnp.int32), axis=1)
    offset = row - jnp.sum(jnp.where(past, tally[None, :], 0), axis=1)
    away = (holder >> 1) ^ chip
    slot = (((away >> 2) & 1) + ((away >> 1) & 1) * 2 + (away & 1) * 4) * (2 * capacity)
    slot = slot + ((holder & 1) ^ core) * capacity + offset
    prompt = prompt_of[0]
    before = (prompt[None, :] == prompt[:, None]) & (row[None, :] < row[:, None])
    rank = prompt * block + jnp.sum(before.astype(jnp.int32), axis=1)
    at_rank = rank[None, :] == row[:, None]
    slot_sorted = jnp.sum(jnp.where(at_rank, slot[None, :], 0), axis=1)
    dest_sorted = jnp.sum(jnp.where(at_rank, row[None, :], 0), axis=1)
    local = jnp.arange(2 * per_device, dtype=jnp.int32)
    local = (me ^ (local // per_device)) * per_device + local % per_device
    own_slot = jnp.sum(jnp.where(local[:, None] == row[None, :], slot[None, :], 0), axis=1)
    spot = jnp.stack([core, group, upper]).astype(jnp.int32)

    packed = half + LANES
    pairs = 2
    whole = lambda *shape: pl.BlockSpec(shape, lambda i, s: (0,) * len(shape))
    cache = pl.BlockSpec((pairs, depth, HD), lambda i, s: (i, 0, 0))
    parts, own_part = pl.pallas_call(
        functools.partial(attend_kernel, heads, pairs),
        out_shape=[
            jax.ShapeDtypeStruct((chips, total // chips, packed), BF),
            jax.ShapeDtypeStruct((2 * per_device, packed), BF),
        ],
        grid_spec=pltpu.PrefetchScalarGridSpec(
            num_scalar_prefetch=1,
            grid=(prompts // pairs,),
            in_specs=[
                pl.BlockSpec((block * pairs, 1), lambda i, s: (i, 0)),
                whole(1, total),
                whole(2 * per_device, 1),
                whole(2 * per_device, 1),
                whole(*slots.shape),
                whole(*new_pairs.shape),
                cache,
                cache,
                cache,
                cache,
                whole(*suffixes.shape),
            ],
            out_specs=[whole(chips, total // chips, packed), whole(2 * per_device, packed)],
            scratch_shapes=[pltpu.VMEM((total, packed), BF)],
        ),
        compiler_params=pltpu.CompilerParams(vmem_limit_bytes=20 << 20),
        name="attend",
    )(
        spot,
        slot_sorted[:, None],
        dest_sorted[None, :],
        own_slot[:, None],
        gens,
        slots,
        new_pairs,
        keys,
        other_keys,
        values,
        other_values,
        suffixes,
    )
    parts = lax.all_to_all(parts, "seq", 0, 0, axis_index_groups=line, tiled=True)
    spread = pl.pallas_call(
        functools.partial(join_kernel, heads),
        out_shape=jax.ShapeDtypeStruct((chips, 2 * per_device, half), BF),
        in_specs=[VMEM] * 2,
        out_specs=VMEM,
        compiler_params=pltpu.CompilerParams(vmem_limit_bytes=8 << 20),
        name="join",
    )(parts, own_part)
    attended = lax.all_to_all(spread, "seq", 0, 0, axis_index_groups=line, tiled=True).reshape(total, half)
    partner = swap(attended, "seq", 1)
    columns = out_weight.shape[1]
    plane = [[(z * 4 + y) * 4 + x for y in range(4) for x in range(4)] for z in range(2)]
    products = pl.pallas_call(
        project_kernel,
        out_shape=jax.ShapeDtypeStruct((16, total // 2, columns), BF),
        in_specs=[SMEM] + [VMEM] * 6,
        out_specs=VMEM,
        compiler_params=pltpu.CompilerParams(vmem_limit_bytes=8 << 20),
        name="project",
    )(spot, attended, partner, *weights)
    products = lax.all_to_all(products, ("tp", "rep"), 0, 0, axis_index_groups=plane, tiled=True)
    keep, send = pl.pallas_call(
        plane_kernel,
        out_shape=[
            jax.ShapeDtypeStruct((total // 2, columns), F32),
            jax.ShapeDtypeStruct((total // 2, columns), BF),
        ],
        in_specs=[SMEM, VMEM],
        out_specs=[VMEM] * 2,
        compiler_params=pltpu.CompilerParams(vmem_limit_bytes=8 << 20),
        name="plane",
    )(spot, products)
    return (keep + swap(send, "tp", 4).astype(F32)).astype(BF)


def solution(mesh):
    in_specs = (
        P("rep", None),
        P("rep", None),
        P("rep", "seq", "tp"),
        P("rep", "seq", None, "tp"),
        P("rep", None, "seq", "tp"),
        P("rep", None, "seq", "tp"),
        P("rep", "seq", None, "tp"),
        P("rep", "seq", None, "tp"),
        P("rep", "seq"),
        P("tp", ("seq", "rep")),
    )
    out_specs = P("tp", ("seq", "rep"))
    return jax.shard_map(body, mesh=mesh, in_specs=in_specs, out_specs=out_specs, check_vma=False)
```

```python
import functools
import math

import jax
import jax.numpy as jnp
from jax import lax
from jax.experimental import pallas as pl
from jax.experimental.pallas import tpu as pltpu
from jax.sharding import PartitionSpec as P


HD = 128
LANES = 128
NEG = -1e30
BF = jnp.bfloat16
F32 = jnp.float32


def swap(x, axis, bit):
    size = lax.axis_size(axis)
    return lax.ppermute(x, axis, [(i, i ^ bit) for i in range(size)])


def dot(a, b):
    return lax.dot_general(a, b, (((1,), (0,)), ((), ())), preferred_element_type=F32)


def dot_t(a, b):
    return lax.dot_general(a, b, (((1,), (1,)), ((), ())), preferred_element_type=F32)


def split_stats(stat):
    hi = stat.astype(BF).astype(F32)
    rest = stat - hi
    mid = rest.astype(BF).astype(F32)
    low = rest - mid
    lane = lax.broadcasted_iota(jnp.int32, stat.shape, 1)
    out = jnp.where(lane < 8, hi, jnp.where(lane < 16, pltpu.roll(mid, 8, 1), pltpu.roll(low, 16, 1)))
    return jnp.where(lane < 24, out, 0.0).astype(BF)


def join_stats(packed):
    x = packed.astype(F32)
    return x + pltpu.roll(x, LANES - 8, 1) + pltpu.roll(x, LANES - 16, 1)


def heads_down(x, heads):
    return jnp.concatenate([x[:, h * HD : (h + 1) * HD] for h in range(heads)], axis=0)


def lanes_of(column, heads, rows):
    lane = lax.broadcasted_iota(jnp.int32, (rows, LANES), 1)
    out = jnp.zeros((rows, LANES), F32)
    for h in range(heads):
        out = jnp.where(lane == h, column[h * rows : (h + 1) * rows], out)
    return out


def one_hot(ids, width, offset=0):
    lane = lax.broadcasted_iota(jnp.int32, (ids.shape[0], width), 1)
    return jnp.where(ids - offset == lane, 1.0, 0.0).astype(BF)


def log_stats(top, mass, factor, heads, rows):
    return split_stats(lanes_of(top * factor + jnp.log2(mass), heads, rows))


def order_kernel(block, slot_rows, spot, counts, prompt, slot_of, rank_of, own_slot):
    core, chip = spot[0], spot[3]
    total = prompt.shape[1]
    capacity = slot_rows
    row = lax.broadcasted_iota(jnp.int32, (1, total), 1)
    end = jnp.int32(0)
    holder = jnp.zeros((1, total), jnp.int32)
    offset = row
    for s in range(counts.shape[1]):
        count = counts[0, s]
        end = end + count
        past = row >= end
        holder = holder + jnp.where(past, 1, 0)
        offset = offset - jnp.where(past, count, 0)
    away = (holder >> 1) ^ chip
    place = ((holder & 1) ^ core) + ((away >> 2) & 1) * 2 + ((away >> 1) & 1) * 4 + (away & 1) * 8
    slot = place * capacity + offset
    lane = lax.broadcasted_iota(jnp.int32, (total, total), 1)
    sub = lax.broadcasted_iota(jnp.int32, (total, total), 0)
    across = jnp.broadcast_to(prompt[...], (total, total))
    down = jnp.sum(jnp.where(lane == sub, across, 0), axis=1, keepdims=True)
    same = across == down
    rank_of[...] = down * block + jnp.sum(jnp.where(same & (lane < sub), 1, 0), axis=1, keepdims=True)
    rank = prompt[...] * block + jnp.sum(jnp.where(same & (sub < lane), 1, 0), axis=0, keepdims=True)
    slot_of[...] = jnp.sum(jnp.where(rank == sub, slot, 0), axis=1, keepdims=True)
    n = own_slot.shape[0]
    local = lax.broadcasted_iota(jnp.int32, (n, total), 0)
    own = n // 2
    local = ((2 * chip + core) ^ (local // own)) * own + local % own
    own_slot[...] = jnp.sum(jnp.where(local == lane[:n], slot, 0), axis=1, keepdims=True)


def attend_kernel(heads, spot, slot_of, rank_of, own_slot, near, far, small, other_small, keys, other_keys, values, other_values, suf, other_suf, out, suffix_out, sorted_rows, queries, fresh_rows):
    core = spot[0]
    width = heads * HD
    factor = HD**-0.5 * math.log2(math.e)
    prompts = keys.shape[0]
    total = slot_of.shape[0]
    rows = total // prompts
    half = near.shape[0]
    own = own_slot.shape[0] // 2
    capacity = small.shape[0] - own

    def pick(ids):
        return (dot(one_hot(ids, half), near[...]) + dot(one_hot(ids, half, half), far[...])).astype(BF)

    ids = slot_of[...]
    q = pick(jnp.concatenate([ids, own_slot[...]], axis=0))
    own_q = q[total:]
    for p in range(prompts):
        for h in range(heads):
            queries[p, h * rows : (h + 1) * rows] = q[p * rows : (p + 1) * rows, h * HD : (h + 1) * HD]
    fresh_rows[...] = dot(one_hot(ids, capacity), small[:capacity]) + dot(
        one_hot(ids, capacity, capacity), other_small[:capacity]
    )

    def score(p):
        q = queries[p]
        return dot_t(q, keys[p]), dot_t(q, other_keys[p])

    def finish(p, scores):
        a, b = scores
        fresh = fresh_rows[p * rows : (p + 1) * rows]
        fresh_k = jnp.concatenate([fresh[:, :HD]] * heads, axis=0)
        fresh_v = jnp.concatenate([fresh[:, HD:]] * heads, axis=0)
        mine = jnp.concatenate([slot_of[p * rows : (p + 1) * rows]] * heads, axis=0) < 2 * capacity
        self_score = jnp.sum(queries[p].astype(F32) * fresh_k, axis=1, keepdims=True)
        self_score = jnp.where(mine, self_score, NEG)
        peak = jnp.max(jnp.maximum(a, b), axis=1, keepdims=True)
        peak = jnp.maximum(peak, self_score)
        a = jnp.exp2((a - peak) * factor)
        b = jnp.exp2((b - peak) * factor)
        self_weight = jnp.exp2((self_score - peak) * factor)
        mass = jnp.sum(a + b, axis=1, keepdims=True) + self_weight
        mixed = dot(a.astype(BF), values[p]) + dot(b.astype(BF), other_values[p])
        mixed = mixed + self_weight.astype(BF).astype(F32) * fresh_v
        mixed = (mixed / mass).astype(BF)
        for h in range(heads):
            sorted_rows[p * rows : (p + 1) * rows, h * HD : (h + 1) * HD] = mixed[h * rows : (h + 1) * rows]
        sorted_rows[p * rows : (p + 1) * rows, width : width + LANES] = log_stats(peak, mass, factor, heads, rows)

    tall = (suf.shape[0] - own) // 2
    span = tall // own

    def suffix_part(rel, cache):
        qs = heads_down(own_q[rel * own : (rel + 1) * own], heads)
        s = dot_t(qs, cache[:tall])
        row = lax.broadcasted_iota(jnp.int32, (own, 1), 0)
        row = jnp.concatenate([row * span] * heads, axis=0)
        length = cache[2 * tall :, :1].astype(F32).astype(jnp.int32)
        length = jnp.concatenate([length] * heads, axis=0)
        t = lax.broadcasted_iota(jnp.int32, s.shape, 1) - row
        s = jnp.where((t >= 0) & (t < length), s, NEG)
        top = jnp.max(s, axis=1, keepdims=True)
        w = jnp.exp2((s - top) * factor)
        m = jnp.sum(w, axis=1, keepdims=True)
        o = (dot(w.astype(BF), cache[tall : 2 * tall]) / m).astype(BF)
        at = pl.ds(pl.multiple_of((core ^ rel) * own, own), own)
        for h in range(heads):
            suffix_out[at, h * HD : (h + 1) * HD] = o[h * own : (h + 1) * own]
        suffix_out[at, width : width + LANES] = log_stats(top, m, factor, heads, own)

    pending = score(0)
    for p in range(prompts):
        following = score(p + 1) if p + 1 < prompts else None
        finish(p, pending)
        if p in (1, 4):
            suffix_part(*((0, suf) if p == 1 else (1, other_suf)))
        pending = following

    place = lax.broadcasted_iota(jnp.int32, (total, total), 1)
    to_row = jnp.where(place == rank_of[...], 1.0, 0.0).astype(BF)
    placed = dot(to_row, sorted_rows[...]).astype(BF)
    n = out.shape[1]
    for i in range(out.shape[0]):
        out[i] = placed[i * n : (i + 1) * n]


def stage_kernel(home, out, landed):
    copy = pltpu.make_async_copy(home, out, landed)
    copy.start()
    copy.wait()


def join_kernel(heads, parts, suffix, out):
    width = heads * HD
    count = parts.shape[0]
    stats = [join_stats(parts[i, :, width : width + LANES]) for i in range(count)]
    stats.append(join_stats(suffix[:, width : width + LANES]))
    top = functools.reduce(jnp.maximum, stats)
    grown = [jnp.exp2(s - top) for s in stats]
    total = functools.reduce(jnp.add, grown)
    share = [e / total for e in grown]
    for h in range(heads):
        cut = slice(h * HD, (h + 1) * HD)
        o = suffix[:, cut].astype(F32) * share[count][:, h : h + 1]
        for i in range(count):
            o = o + parts[i, :, cut].astype(F32) * share[i][:, h : h + 1]
        o = o.astype(BF)
        for i in range(out.shape[0]):
            out[i, :, cut] = o


def project_kernel(spot, mine, partner, w0, w1, w2, w3, out):
    core, group = spot[0], spot[1]
    out[...] = jnp.zeros_like(out)
    depth = mine.shape[1]
    near = pl.ds(pl.multiple_of(core * depth, depth), depth)
    far = pl.ds(pl.multiple_of((1 - core) * depth, depth), depth)
    n = out.shape[1]
    for rel, w in enumerate((w0, w1, w2, w3)):
        y = (dot(mine[...], w[near, :]) + dot(partner[...], w[far, :])).astype(BF)
        for high in range(2):
            out[((group % 2) * 2 + high) * 4 + (group ^ rel)] = y[high * n : (high + 1) * n]


def plane_kernel(spot, parts, keep, send):
    sums = []
    for top in range(2):
        terms = [parts[y * 4 + top * 2 + g].astype(F32) for y in range(4) for g in range(2)]
        sums.append(functools.reduce(jnp.add, terms))
    upper = spot[2] == 1
    keep[...] = jnp.where(upper, sums[1], sums[0])
    send[...] = jnp.where(upper, sums[0], sums[1]).astype(BF)


VMEM = pl.BlockSpec(memory_space=pltpu.VMEM)
SMEM = pl.BlockSpec(memory_space=pltpu.SMEM)


def body(counts, prompt_of, queries, new_kv, prompt_keys, prompt_values, suffix_keys, suffix_values, gen_len, out_weight):
    me = lax.axis_index("seq")
    core, chip = me & 1, me >> 1
    group = lax.axis_index("rep")
    upper = lax.axis_index("tp") >> 2
    capacity, width = queries.shape[1:]
    heads = width // HD // 2
    half = heads * HD
    per_device = gen_len.shape[1]
    seq_count = lax.axis_size("seq")
    chips = seq_count // 2
    total = per_device * seq_count
    prompts, _ = prompt_keys.shape[1:3]
    block = total // prompts
    line = [[2 * i + c for i in range(chips)] for c in range(2)]

    halves = queries[0][:, :half], queries[0][:, half:]
    low = core == 0
    mine = jnp.where(low, halves[0], halves[1])
    theirs = jnp.where(low, halves[1], halves[0])
    far_chip = swap(mine, "seq", 8)
    far_cross = swap(theirs, "seq", 9)
    near_core = swap(theirs, "seq", 1)
    slots = jnp.concatenate([mine, near_core, far_chip, far_cross], axis=0)

    spot = jnp.stack([core, group, upper, chip]).astype(jnp.int32)
    new_rows, sk, sv, gens = new_kv[0], suffix_keys[0], suffix_values[0], gen_len[0]
    keys, values, weight, tally, prompt = prompt_keys[0], prompt_values[0], out_weight, counts, prompt_of
    small = jnp.pad(new_rows.reshape(capacity, 2 * HD), ((0, per_device), (0, 0)))
    lengths = jnp.broadcast_to(gens.astype(BF)[:, None], (per_device, HD))
    suffix = jnp.concatenate([sk.reshape(-1, HD), sv.reshape(-1, HD), lengths], axis=0)
    slots = jnp.concatenate([slots, swap(slots, "seq", 4)], axis=0)
    far_slots = swap(slots, "seq", 2)
    other_small = swap(small, "seq", 1)
    other_suffix = swap(suffix, "seq", 1)
    other_keys = swap(keys, "seq", 1)
    home = pltpu.with_memory_space_constraint(values, pltpu.HBM)
    staged = pl.pallas_call(
        stage_kernel,
        out_shape=jax.ShapeDtypeStruct(values.shape, BF),
        in_specs=[pl.BlockSpec(memory_space=pltpu.HBM)],
        out_specs=VMEM,
        scratch_shapes=[pltpu.SemaphoreType.DMA],
        compiler_params=pltpu.CompilerParams(vmem_limit_bytes=8 << 20),
        name="stage",
    )(home)
    other_values = swap(values, "seq", 1)
    weights = [weight]
    for bit in (1, 2, 3):
        weights.append(swap(weight, "rep", bit))
    tables = pl.pallas_call(
        functools.partial(order_kernel, block, capacity),
        out_shape=[
            jax.ShapeDtypeStruct((total, 1), jnp.int32),
            jax.ShapeDtypeStruct((total, 1), jnp.int32),
            jax.ShapeDtypeStruct((2 * per_device, 1), jnp.int32),
        ],
        in_specs=[SMEM, SMEM, VMEM],
        out_specs=[VMEM] * 3,
        compiler_params=pltpu.CompilerParams(vmem_limit_bytes=8 << 20),
        cost_estimate=pl.CostEstimate(flops=1 << 20, bytes_accessed=1 << 18, transcendentals=0),
        name="order",
    )(spot, tally, prompt)

    packed = half + LANES
    parts, own_part = pl.pallas_call(
        functools.partial(attend_kernel, heads),
        out_shape=[
            jax.ShapeDtypeStruct((chips, total // chips, packed), BF),
            jax.ShapeDtypeStruct((2 * per_device, packed), BF),
        ],
        in_specs=[SMEM] + [VMEM] * 13,
        out_specs=[VMEM] * 2,
        scratch_shapes=[
            pltpu.VMEM((total, packed), BF),
            pltpu.VMEM((prompts, block * heads, HD), BF),
            pltpu.VMEM((total, 2 * HD), F32),
        ],
        compiler_params=pltpu.CompilerParams(vmem_limit_bytes=24 << 20),
        name="attend",
    )(
        spot,
        *tables,
        slots,
        far_slots,
        small,
        other_small,
        keys,
        other_keys,
        staged,
        other_values,
        suffix,
        other_suffix,
    )
    parts = lax.all_to_all(parts, "seq", 0, 0, axis_index_groups=line, tiled=True)
    spread = pl.pallas_call(
        functools.partial(join_kernel, heads),
        out_shape=jax.ShapeDtypeStruct((chips, 2 * per_device, half), BF),
        in_specs=[VMEM] * 2,
        out_specs=VMEM,
        compiler_params=pltpu.CompilerParams(vmem_limit_bytes=8 << 20),
        name="join",
    )(parts, own_part)
    attended = lax.all_to_all(spread, "seq", 0, 0, axis_index_groups=line, tiled=True).reshape(total, half)
    partner = swap(attended, "seq", 1)
    columns = out_weight.shape[1]
    plane = [[(z * 4 + y) * 4 + x for y in range(4) for x in range(4)] for z in range(2)]
    products = pl.pallas_call(
        project_kernel,
        out_shape=jax.ShapeDtypeStruct((16, total // 2, columns), BF),
        in_specs=[SMEM] + [VMEM] * 6,
        out_specs=VMEM,
        compiler_params=pltpu.CompilerParams(vmem_limit_bytes=8 << 20),
        name="project",
    )(spot, attended, partner, *weights)
    products = lax.all_to_all(products, ("tp", "rep"), 0, 0, axis_index_groups=plane, tiled=True)
    keep, send = pl.pallas_call(
        plane_kernel,
        out_shape=[
            jax.ShapeDtypeStruct((total // 2, columns), F32),
            jax.ShapeDtypeStruct((total // 2, columns), BF),
        ],
        in_specs=[SMEM, VMEM],
        out_specs=[VMEM] * 2,
        compiler_params=pltpu.CompilerParams(vmem_limit_bytes=8 << 20),
        name="plane",
    )(spot, products)
    return (keep + swap(send, "tp", 4).astype(F32)).astype(BF)


def solution(mesh):
    in_specs = (
        P("rep", None),
        P("rep", None),
        P("rep", "seq", "tp"),
        P("rep", "seq", None, "tp"),
        P("rep", None, "seq", "tp"),
        P("rep", None, "seq", "tp"),
        P("rep", "seq", None, "tp"),
        P("rep", "seq", None, "tp"),
        P("rep", "seq"),
        P("tp", ("seq", "rep")),
    )
    out_specs = P("tp", ("seq", "rep"))
    return jax.shard_map(body, mesh=mesh, in_specs=in_specs, out_specs=out_specs, check_vma=False)
```

```python
import functools
import math

import jax
import jax.numpy as jnp
from jax import lax
from jax.experimental import pallas as pl
from jax.experimental.pallas import tpu as pltpu
from jax.sharding import PartitionSpec as P


HD = 128
LANES = 128
NEG = -1e30
BF = jnp.bfloat16
F32 = jnp.float32


def swap(x, axis, bit):
    size = lax.axis_size(axis)
    return lax.ppermute(x, axis, [(i, i ^ bit) for i in range(size)])


def dot(a, b):
    return lax.dot_general(a, b, (((1,), (0,)), ((), ())), preferred_element_type=F32)


def dot_t(a, b):
    return lax.dot_general(a, b, (((1,), (1,)), ((), ())), preferred_element_type=F32)


def split_stats(stat):
    hi = stat.astype(BF).astype(F32)
    rest = stat - hi
    mid = rest.astype(BF).astype(F32)
    low = rest - mid
    lane = lax.broadcasted_iota(jnp.int32, stat.shape, 1)
    out = jnp.where(lane < 8, hi, jnp.where(lane < 16, pltpu.roll(mid, 8, 1), pltpu.roll(low, 16, 1)))
    return jnp.where(lane < 24, out, 0.0).astype(BF)


def join_stats(packed):
    x = packed.astype(F32)
    return x + pltpu.roll(x, LANES - 8, 1) + pltpu.roll(x, LANES - 16, 1)


def heads_down(x, heads):
    return jnp.concatenate([x[:, h * HD : (h + 1) * HD] for h in range(heads)], axis=0)


def lanes_of(column, heads, rows):
    lane = lax.broadcasted_iota(jnp.int32, (rows, LANES), 1)
    out = jnp.zeros((rows, LANES), F32)
    for h in range(heads):
        out = jnp.where(lane == h, column[h * rows : (h + 1) * rows], out)
    return out


def one_hot(ids, width, offset=0):
    lane = lax.broadcasted_iota(jnp.int32, (ids.shape[0], width), 1)
    return jnp.where(ids - offset == lane, 1.0, 0.0).astype(BF)


def log_stats(top, mass, factor, heads, rows):
    return split_stats(lanes_of(top * factor + jnp.log2(mass), heads, rows))


def order_kernel(block, slot_rows, spot, counts, prompt, slot_of, rank_of, own_slot):
    core, chip = spot[0], spot[3]
    total = prompt.shape[1]
    capacity = slot_rows
    row = lax.broadcasted_iota(jnp.int32, (1, total), 1)
    end = jnp.int32(0)
    holder = jnp.zeros((1, total), jnp.int32)
    offset = row
    for s in range(counts.shape[1]):
        count = counts[0, s]
        end = end + count
        past = row >= end
        holder = holder + jnp.where(past, 1, 0)
        offset = offset - jnp.where(past, count, 0)
    away = (holder >> 1) ^ chip
    place = ((holder & 1) ^ core) + ((away >> 2) & 1) * 2 + ((away >> 1) & 1) * 4 + (away & 1) * 8
    slot = place * capacity + offset
    lane = lax.broadcasted_iota(jnp.int32, (total, total), 1)
    sub = lax.broadcasted_iota(jnp.int32, (total, total), 0)
    across = jnp.broadcast_to(prompt[...], (total, total))
    down = jnp.sum(jnp.where(lane == sub, across, 0), axis=1, keepdims=True)
    same = across == down
    rank_of[...] = down * block + jnp.sum(jnp.where(same & (lane < sub), 1, 0), axis=1, keepdims=True)
    rank = prompt[...] * block + jnp.sum(jnp.where(same & (sub < lane), 1, 0), axis=0, keepdims=True)
    slot_of[...] = jnp.sum(jnp.where(rank == sub, slot, 0), axis=1, keepdims=True)
    n = own_slot.shape[0]
    local = lax.broadcasted_iota(jnp.int32, (n, total), 0)
    own = n // 2
    local = ((2 * chip + core) ^ (local // own)) * own + local % own
    own_slot[...] = jnp.sum(jnp.where(local == lane[:n], slot, 0), axis=1, keepdims=True)


def attend_kernel(heads, spot, slot_of, rank_of, own_slot, near, far, small, other_small, keys, other_keys, values, other_values, suf, other_suf, out, suffix_out, sorted_rows, queries, fresh_rows):
    core = spot[0]
    width = heads * HD
    factor = HD**-0.5 * math.log2(math.e)
    prompts = keys.shape[0]
    total = slot_of.shape[0]
    rows = total // prompts
    half = near.shape[0]
    own = own_slot.shape[0] // 2
    capacity = small.shape[0] - own

    def pick(ids):
        return (dot(one_hot(ids, half), near[...]) + dot(one_hot(ids, half, half), far[...])).astype(BF)

    ids = slot_of[...]
    q = pick(jnp.concatenate([ids, own_slot[...]], axis=0))
    own_q = q[total:]
    for p in range(prompts):
        for h in range(heads):
            queries[p, h * rows : (h + 1) * rows] = q[p * rows : (p + 1) * rows, h * HD : (h + 1) * HD]
    fresh_rows[...] = dot(one_hot(ids, capacity), small[:capacity]) + dot(
        one_hot(ids, capacity, capacity), other_small[:capacity]
    )

    def score(p):
        q = queries[p]
        return dot_t(q, keys[p]), dot_t(q, other_keys[p])

    def finish(p, scores):
        a, b = scores
        fresh = fresh_rows[p * rows : (p + 1) * rows]
        fresh_k = jnp.concatenate([fresh[:, :HD]] * heads, axis=0)
        fresh_v = jnp.concatenate([fresh[:, HD:]] * heads, axis=0)
        mine = jnp.concatenate([slot_of[p * rows : (p + 1) * rows]] * heads, axis=0) < 2 * capacity
        self_score = jnp.sum(queries[p].astype(F32) * fresh_k, axis=1, keepdims=True)
        self_score = jnp.where(mine, self_score, NEG)
        peak = jnp.max(jnp.maximum(a, b), axis=1, keepdims=True)
        peak = jnp.maximum(peak, self_score)
        a = jnp.exp2((a - peak) * factor)
        b = jnp.exp2((b - peak) * factor)
        self_weight = jnp.exp2((self_score - peak) * factor)
        mass = jnp.sum(a + b, axis=1, keepdims=True) + self_weight
        mixed = dot(a.astype(BF), values[p]) + dot(b.astype(BF), other_values[p])
        mixed = mixed + self_weight.astype(BF).astype(F32) * fresh_v
        mixed = (mixed / mass).astype(BF)
        for h in range(heads):
            sorted_rows[p * rows : (p + 1) * rows, h * HD : (h + 1) * HD] = mixed[h * rows : (h + 1) * rows]
        sorted_rows[p * rows : (p + 1) * rows, width : width + LANES] = log_stats(peak, mass, factor, heads, rows)

    tall = (suf.shape[0] - own) // 2
    span = tall // own

    def suffix_part(rel, cache):
        qs = heads_down(own_q[rel * own : (rel + 1) * own], heads)
        s = dot_t(qs, cache[:tall])
        row = lax.broadcasted_iota(jnp.int32, (own, 1), 0)
        row = jnp.concatenate([row * span] * heads, axis=0)
        length = cache[2 * tall :, :1].astype(F32).astype(jnp.int32)
        length = jnp.concatenate([length] * heads, axis=0)
        t = lax.broadcasted_iota(jnp.int32, s.shape, 1) - row
        s = jnp.where((t >= 0) & (t < length), s, NEG)
        top = jnp.max(s, axis=1, keepdims=True)
        w = jnp.exp2((s - top) * factor)
        m = jnp.sum(w, axis=1, keepdims=True)
        o = (dot(w.astype(BF), cache[tall : 2 * tall]) / m).astype(BF)
        at = pl.ds(pl.multiple_of((core ^ rel) * own, own), own)
        for h in range(heads):
            suffix_out[at, h * HD : (h + 1) * HD] = o[h * own : (h + 1) * own]
        suffix_out[at, width : width + LANES] = log_stats(top, m, factor, heads, own)

    pending = score(0)
    for p in range(prompts):
        following = score(p + 1) if p + 1 < prompts else None
        finish(p, pending)
        if p in (1, 4):
            suffix_part(*((0, suf) if p == 1 else (1, other_suf)))
        pending = following

    place = lax.broadcasted_iota(jnp.int32, (total, total), 1)
    to_row = jnp.where(place == rank_of[...], 1.0, 0.0).astype(BF)
    placed = dot(to_row, sorted_rows[...]).astype(BF)
    n = out.shape[1]
    for i in range(out.shape[0]):
        out[i] = placed[i * n : (i + 1) * n]


def stage_kernel(home, out, landed):
    copy = pltpu.make_async_copy(home, out, landed)
    copy.start()
    copy.wait()


def join_kernel(heads, parts, suffix, out):
    width = heads * HD
    count = parts.shape[0]
    stats = [join_stats(parts[i, :, width : width + LANES]) for i in range(count)]
    stats.append(join_stats(suffix[:, width : width + LANES]))
    top = functools.reduce(jnp.maximum, stats)
    grown = [jnp.exp2(s - top) for s in stats]
    total = functools.reduce(jnp.add, grown)
    share = [e / total for e in grown]
    for h in range(heads):
        cut = slice(h * HD, (h + 1) * HD)
        o = suffix[:, cut].astype(F32) * share[count][:, h : h + 1]
        for i in range(count):
            o = o + parts[i, :, cut].astype(F32) * share[i][:, h : h + 1]
        o = o.astype(BF)
        for i in range(out.shape[0]):
            out[i, :, cut] = o


def project_kernel(spot, mine, partner, home, w1, w2, w3, out, w0, landed):
    core, group = spot[0], spot[1]
    fetch = pltpu.make_async_copy(home, w0, landed)
    fetch.start()
    out[...] = jnp.zeros_like(out)
    depth = mine.shape[1]
    near = pl.ds(pl.multiple_of(core * depth, depth), depth)
    far = pl.ds(pl.multiple_of((1 - core) * depth, depth), depth)
    n = out.shape[1]
    for rel, w in ((1, w1), (2, w2), (3, w3), (0, w0)):
        if rel == 0:
            fetch.wait()
        y = (dot(mine[...], w[near, :]) + dot(partner[...], w[far, :])).astype(BF)
        for high in range(2):
            out[((group % 2) * 2 + high) * 4 + (group ^ rel)] = y[high * n : (high + 1) * n]


def plane_kernel(spot, parts, keep, send):
    sums = []
    for top in range(2):
        terms = [parts[y * 4 + top * 2 + g].astype(F32) for y in range(4) for g in range(2)]
        sums.append(functools.reduce(jnp.add, terms))
    upper = spot[2] == 1
    keep[...] = jnp.where(upper, sums[1], sums[0])
    send[...] = jnp.where(upper, sums[0], sums[1]).astype(BF)


VMEM = pl.BlockSpec(memory_space=pltpu.VMEM)
SMEM = pl.BlockSpec(memory_space=pltpu.SMEM)


def body(counts, prompt_of, queries, new_kv, prompt_keys, prompt_values, suffix_keys, suffix_values, gen_len, out_weight):
    me = lax.axis_index("seq")
    core, chip = me & 1, me >> 1
    group = lax.axis_index("rep")
    upper = lax.axis_index("tp") >> 2
    capacity, width = queries.shape[1:]
    heads = width // HD // 2
    half = heads * HD
    per_device = gen_len.shape[1]
    seq_count = lax.axis_size("seq")
    chips = seq_count // 2
    total = per_device * seq_count
    prompts, _ = prompt_keys.shape[1:3]
    block = total // prompts
    line = [[2 * i + c for i in range(chips)] for c in range(2)]

    halves = queries[0][:, :half], queries[0][:, half:]
    low = core == 0
    mine = jnp.where(low, halves[0], halves[1])
    theirs = jnp.where(low, halves[1], halves[0])
    far_chip = swap(mine, "seq", 8)
    far_cross = swap(theirs, "seq", 9)
    near_core = swap(theirs, "seq", 1)
    slots = jnp.concatenate([mine, near_core, far_chip, far_cross], axis=0)

    spot = jnp.stack([core, group, upper, chip]).astype(jnp.int32)
    new_rows, sk, sv, gens = new_kv[0], suffix_keys[0], suffix_values[0], gen_len[0]
    keys, values, weight, tally, prompt = prompt_keys[0], prompt_values[0], out_weight, counts, prompt_of
    small = jnp.pad(new_rows.reshape(capacity, 2 * HD), ((0, per_device), (0, 0)))
    lengths = jnp.broadcast_to(gens.astype(BF)[:, None], (per_device, HD))
    suffix = jnp.concatenate([sk.reshape(-1, HD), sv.reshape(-1, HD), lengths], axis=0)
    slots = jnp.concatenate([slots, swap(slots, "seq", 4)], axis=0)
    far_slots = swap(slots, "seq", 2)
    other_small = swap(small, "seq", 1)
    other_suffix = swap(suffix, "seq", 1)
    other_keys = swap(keys, "seq", 1)
    home = pltpu.with_memory_space_constraint(values, pltpu.HBM)
    staged = pl.pallas_call(
        stage_kernel,
        out_shape=jax.ShapeDtypeStruct(values.shape, BF),
        in_specs=[pl.BlockSpec(memory_space=pltpu.HBM)],
        out_specs=VMEM,
        scratch_shapes=[pltpu.SemaphoreType.DMA],
        compiler_params=pltpu.CompilerParams(vmem_limit_bytes=8 << 20),
        name="stage",
    )(home)
    other_values = swap(values, "seq", 1)
    weights = [weight]
    for bit in (1, 2, 3):
        weights.append(swap(weight, "rep", bit))
    tables = pl.pallas_call(
        functools.partial(order_kernel, block, capacity),
        out_shape=[
            jax.ShapeDtypeStruct((total, 1), jnp.int32),
            jax.ShapeDtypeStruct((total, 1), jnp.int32),
            jax.ShapeDtypeStruct((2 * per_device, 1), jnp.int32),
        ],
        in_specs=[SMEM, SMEM, VMEM],
        out_specs=[VMEM] * 3,
        compiler_params=pltpu.CompilerParams(vmem_limit_bytes=8 << 20),
        cost_estimate=pl.CostEstimate(flops=1 << 20, bytes_accessed=1 << 18, transcendentals=0),
        name="order",
    )(spot, tally, prompt)

    packed = half + LANES
    parts, own_part = pl.pallas_call(
        functools.partial(attend_kernel, heads),
        out_shape=[
            jax.ShapeDtypeStruct((chips, total // chips, packed), BF),
            jax.ShapeDtypeStruct((2 * per_device, packed), BF),
        ],
        in_specs=[SMEM] + [VMEM] * 13,
        out_specs=[VMEM] * 2,
        scratch_shapes=[
            pltpu.VMEM((total, packed), BF),
            pltpu.VMEM((prompts, block * heads, HD), BF),
            pltpu.VMEM((total, 2 * HD), F32),
        ],
        compiler_params=pltpu.CompilerParams(vmem_limit_bytes=24 << 20),
        name="attend",
    )(
        spot,
        *tables,
        slots,
        far_slots,
        small,
        other_small,
        keys,
        other_keys,
        staged,
        other_values,
        suffix,
        other_suffix,
    )
    parts = lax.all_to_all(parts, "seq", 0, 0, axis_index_groups=line, tiled=True)
    spread = pl.pallas_call(
        functools.partial(join_kernel, heads),
        out_shape=jax.ShapeDtypeStruct((chips, 2 * per_device, half), BF),
        in_specs=[VMEM] * 2,
        out_specs=VMEM,
        compiler_params=pltpu.CompilerParams(vmem_limit_bytes=8 << 20),
        name="join",
    )(parts, own_part)
    attended = lax.all_to_all(spread, "seq", 0, 0, axis_index_groups=line, tiled=True)
    attended = attended.reshape(total, half)
    partner = swap(attended, "seq", 1)
    columns = out_weight.shape[1]
    plane = [[(z * 4 + y) * 4 + x for y in range(4) for x in range(4)] for z in range(2)]
    products = pl.pallas_call(
        project_kernel,
        out_shape=jax.ShapeDtypeStruct((16, total // 2, columns), BF),
        in_specs=[SMEM] + [VMEM] * 2 + [pl.BlockSpec(memory_space=pltpu.HBM)] + [VMEM] * 3,
        out_specs=VMEM,
        scratch_shapes=[pltpu.VMEM(out_weight.shape, BF), pltpu.SemaphoreType.DMA],
        compiler_params=pltpu.CompilerParams(vmem_limit_bytes=8 << 20),
        name="project",
    )(spot, attended, partner, pltpu.with_memory_space_constraint(out_weight, pltpu.HBM), *weights[1:])
    products = lax.all_to_all(products, ("tp", "rep"), 0, 0, axis_index_groups=plane, tiled=True)
    keep, send = pl.pallas_call(
        plane_kernel,
        out_shape=[
            jax.ShapeDtypeStruct((total // 2, columns), F32),
            jax.ShapeDtypeStruct((total // 2, columns), BF),
        ],
        in_specs=[SMEM, VMEM],
        out_specs=[VMEM] * 2,
        compiler_params=pltpu.CompilerParams(vmem_limit_bytes=8 << 20),
        name="plane",
    )(spot, products)
    return (keep + swap(send, "tp", 4).astype(F32)).astype(BF)


def solution(mesh):
    in_specs = (
        P("rep", None),
        P("rep", None),
        P("rep", "seq", "tp"),
        P("rep", "seq", None, "tp"),
        P("rep", None, "seq", "tp"),
        P("rep", None, "seq", "tp"),
        P("rep", "seq", None, "tp"),
        P("rep", "seq", None, "tp"),
        P("rep", "seq"),
        P("tp", ("seq", "rep")),
    )
    out_specs = P("tp", ("seq", "rep"))
    return jax.shard_map(body, mesh=mesh, in_specs=in_specs, out_specs=out_specs, check_vma=False)
```
